256 devices in a mesh: bus: 64 (over z, y, core), tm: 4 (over x).
Axes of the slice: x: 4, y: 4, z: 8, core: 2. Of those that a mesh axis runs over, the one named last changes fastest.
Arguments:
- features: bfloat16 [8192, 64, 128], P('bus', 'tm'), may hold values from -6 to 6
- couplings: bfloat16 [128, 8, 64, 64], P('bus'), may hold values from -0.25 to 0.25
- neighbors: int32 [128, 8], P('bus'), may hold values from 0 to 127, as said below
- w_graph: bfloat16 [128, 128], replicated, may hold values from -0.5 to 0.5
- kernel_taps: bfloat16 [64, 128], replicated, may hold values from -0.3984375 to 0.3984375
- w_out: bfloat16 [128, 128], replicated, may hold values from -0.5 to 0.5
- cotangent: bfloat16 [8192, 64, 128], P('bus', 'tm'), may hold values from -6 to 6
Outputs:
- grad_features: bfloat16 [8192, 64, 128], P('bus', 'tm')
- grad_graph: float32 [128, 128], replicated
- grad_out: float32 [128, 128], replicated
- grad_taps: float32 [64, 128], replicated
The draws below stay inside these ranges and needn't reach their ends.
Inputs may be any that keep to these rules, and one draw needn't show every extreme that they name: neighbors[i, 0] = i. Counting 2 blocks to each index of bus, every entry of block i names a block of the same index, one of the last 1 block of the index before, or one of the first 1 block of the index after.
All inputs are finite; a program needn't handle non-finite values.
Results may differ from the reference program's by a relative error of at most 0.0067.
Values may be sent and summed in bfloat16 or wider, within the bound.
A program may use at most 64 MiB of HBM per device.

```python
import math
import jax
import jax.numpy as jnp
from jax import lax

C = 128
BUSES_PER_BLOCK = 64
COUPLING_SLOTS = 8
BORDER_BLOCKS = 1
BLOCKS_PER_SHARD = 2
TOTAL_BLOCKS = 128
NB = 8192
TIME = 64


def draw_neighbors(key, part):
    block_ids = jnp.arange(TOTAL_BLOCKS, dtype=jnp.int32)
    owner = block_ids // BLOCKS_PER_SHARD
    slot_offsets = jax.random.randint(key, (TOTAL_BLOCKS, COUPLING_SLOTS - 1), -BORDER_BLOCKS, BLOCKS_PER_SHARD + BORDER_BLOCKS, dtype=jnp.int32)
    target = jnp.clip(owner[:, None] * BLOCKS_PER_SHARD + slot_offsets, 0, TOTAL_BLOCKS - 1)
    return jnp.concatenate([block_ids[:, None], target], axis=1).astype(jnp.int32)


def block_scale(key, shape, pieces, least, high):
    gain, own = 1.0, jax.random.fold_in(key, 6)
    for axis_at, parts in pieces:
        heights = jnp.exp(jax.random.uniform(jax.random.fold_in(own, axis_at), (parts,), jnp.float32, least / len(pieces), high / len(pieces)))
        gain = gain * jnp.repeat(heights, shape[axis_at] // parts).reshape([-1 if axis == axis_at else 1 for axis in range(len(shape))])
    return gain


def noise(own_key, shape, width, most, pieces=(), held_as=jnp.bfloat16):
    loudness = block_scale(own_key, shape, pieces, -0.22, 0.18) if pieces else 1.0
    values = jax.random.normal(own_key, shape, jnp.float32) * width * loudness
    return jnp.minimum(jnp.maximum(values, -most), most).astype(held_as)


def setup_inputs(seed: int = 0) -> dict:
    key_of = jax.random.split(jax.random.key(seed), 8)
    return {
        "features": noise(key_of[0], (NB, TIME, C), 1.0, 6.0, ((0, 64), (1, 4))),
        "couplings": noise(key_of[1], (TOTAL_BLOCKS, COUPLING_SLOTS, BUSES_PER_BLOCK, BUSES_PER_BLOCK), (BUSES_PER_BLOCK * COUPLING_SLOTS) ** -0.5, 0.25, ((0, 64),)),
        "neighbors": draw_neighbors(jax.random.fold_in(key_of[7], 71), 0),
        "w_graph": noise(key_of[3], (C, C), C ** -0.5, 0.5),
        "kernel_taps": noise(key_of[4], (TIME, C), 0.07, 0.3984375),
        "w_out": noise(key_of[5], (C, C), C ** -0.5, 0.5),
        "cotangent": noise(key_of[6], (NB, TIME, C), 1.0, 6.0, ((0, 64), (1, 4))),
    }


def rounded(values):
    return lax.optimization_barrier(values.astype(jnp.bfloat16)).astype(jnp.float32)

def toeplitz_table(kernel_taps):
    length = kernel_taps.shape[0]
    row_ids = jnp.arange(length, dtype=jnp.int32)
    lagged = row_ids[:, None] - row_ids[None, :]
    picked = jnp.take(kernel_taps.T, jnp.clip(lagged, 0, length - 1), axis=1)
    return jnp.where(lagged[None] >= 0, picked, jnp.zeros_like(picked))

def lag_sums(lag_table):
    channels = lag_table.shape[0]
    length = lag_table.shape[1]
    flipped = lag_table[:, :, ::-1]
    padded = jnp.pad(flipped, ((0, 0), (0, 0), (0, 1)))
    flat_view = padded.reshape(channels, length * (length + 1))
    window = flat_view[:, length - 1:length - 1 + length * length].reshape(channels, length, length)
    row_ids = jnp.arange(length, dtype=jnp.int32)
    lag_mask = row_ids[None, :, None] >= row_ids[None, None, :]
    return lax.optimization_barrier(jnp.sum(jnp.where(lag_mask, window, jnp.zeros_like(window)), axis=1)).T

def silu_slope(pre_act):
    sigmoid_val = jax.nn.sigmoid(pre_act)
    return sigmoid_val * (1.0 + pre_act * (1.0 - sigmoid_val))

def reference(features, couplings, neighbors, w_graph, kernel_taps, w_out, cotangent):
    flat_len = TIME * C
    blocks_in = features.reshape(TOTAL_BLOCKS, BUSES_PER_BLOCK, flat_len)

    def graph_one(block_index):
        gathered = blocks_in[neighbors[block_index]].astype(jnp.float32)
        return jnp.einsum('kab,kbn->an', couplings[block_index].astype(jnp.float32), gathered).astype(jnp.bfloat16)
    mixed_blocks = lax.map(graph_one, jnp.arange(TOTAL_BLOCKS, dtype=jnp.int32))
    lag_table = toeplitz_table(kernel_taps).astype(jnp.float32)
    graph_weight = w_graph.astype(jnp.float32)
    out_weight = w_out.astype(jnp.float32)
    cot_blocks = cotangent.reshape(TOTAL_BLOCKS, BUSES_PER_BLOCK, TIME, C)

    def pointwise(pair):
        mixed_one, cot_one = pair
        mixed_one = mixed_one.reshape(BUSES_PER_BLOCK, TIME, C).astype(jnp.float32)
        pre_act = jnp.einsum('btc,cd->btd', mixed_one, graph_weight)
        activated = rounded(jax.nn.silu(pre_act))
        convolved_rows = rounded(jnp.einsum('cts,bsc->btc', lag_table, activated))
        cot_float = cot_one.astype(jnp.float32)
        part_out = jnp.einsum('btc,btd->cd', convolved_rows, cot_float)
        grad_conv = rounded(jnp.einsum('btd,cd->btc', cot_float, out_weight))
        part_taps = lag_sums(jnp.einsum('btc,bsc->cts', grad_conv, activated))
        grad_act = rounded(jnp.einsum('cts,btc->bsc', lag_table, grad_conv))
        grad_pre = rounded(grad_act * silu_slope(pre_act))
        part_graph = jnp.einsum('btc,btd->cd', mixed_one, grad_pre)
        grad_mixed = jnp.einsum('btd,cd->btc', grad_pre, graph_weight).astype(jnp.bfloat16)
        return (grad_mixed.reshape(BUSES_PER_BLOCK, flat_len), part_graph, part_out, part_taps)
    grad_mixed, parts_graph, parts_out, parts_taps = lax.map(pointwise, (mixed_blocks, cot_blocks))

    def spread_one(total_sum, block_index):
        contrib = jnp.einsum('kab,an->kbn', couplings[block_index].astype(jnp.float32), grad_mixed[block_index].astype(jnp.float32))
        return (total_sum.at[neighbors[block_index]].add(contrib), None)
    start_sum = jnp.zeros((TOTAL_BLOCKS, BUSES_PER_BLOCK, flat_len), jnp.float32)
    total_sum, unused = lax.scan(spread_one, start_sum, jnp.arange(TOTAL_BLOCKS, dtype=jnp.int32))
    grad_features = (total_sum.reshape(NB, TIME, C) + cotangent.astype(jnp.float32)).astype(jnp.bfloat16)
    grad_scale = 1.0 / math.sqrt(NB * TIME)
    grad_graph = lax.optimization_barrier(jnp.sum(parts_graph, axis=0)) * grad_scale
    grad_out = lax.optimization_barrier(jnp.sum(parts_out, axis=0)) * grad_scale
    grad_taps = lax.optimization_barrier(jnp.sum(parts_taps, axis=0)) * grad_scale
    return (grad_features, grad_graph, grad_out, grad_taps)
```

```python
import functools
import math

import jax
import jax.numpy as jnp
import ml_dtypes
import numpy as np
from jax import lax
from jax.experimental import pallas as pl
from jax.experimental.pallas import tpu as pltpu
from jax.sharding import PartitionSpec as P

CORES = 2
CHIPS_Y = 4
MESH = pl.DeviceIdType.MESH
F32 = jnp.float32
BF16 = jnp.bfloat16


def dft_tables(length):
    freq = 2 * np.arange(length)[:, None] + 1
    angle = np.pi * freq * np.arange(length)[None, :] / (2 * length)
    forward = np.concatenate([np.cos(angle), -np.sin(angle)], axis=0)
    inverse = forward.T / length

    def parts(table):
        high = table.astype(ml_dtypes.bfloat16)
        low = (table - high.astype(np.float64)).astype(ml_dtypes.bfloat16)
        return high, low

    f_high, f_low = parts(forward)
    i_high, i_low = parts(inverse)
    return (
        np.concatenate([f_high, f_low], axis=1),
        np.concatenate([i_high, i_high, i_low], axis=1),
    )


def split(value):
    high = value.astype(BF16)
    low = (value - high.astype(F32)).astype(BF16)
    return high, low


def mm(a, b):
    return jnp.dot(a, b, preferred_element_type=F32)


def mm_t(a, b, da, db):
    return lax.dot_general(a, b, (((da,), (db,)), ((), ())), preferred_element_type=F32)


def kernel(
    sizes,
    feat,
    cot,
    coup,
    nbr,
    wg,
    taps,
    wo,
    fwd_tab,
    inv_tab,
    grad_feat,
    grad_graph,
    grad_out,
    grad_taps,
    fx,
    ft,
    perm,
    m_mat,
    mt_mat,
    mixed,
    slope,
    act_t,
    act_b,
    act_w,
    cot_v,
    cot_w,
    gc_w,
    g_freq,
    kr,
    ki,
    grad_w,
    grad_b,
    own,
    send_prev,
    send_next,
    from_prev,
    from_next,
    out_v,
    red_a,
    rs_a,
    y_a,
    z_a,
    sum_a,
    red_b,
    rs_b,
    y_b,
    z_b,
    sum_b,
    loc_sem,
    out_sem,
    halo_s,
    halo_r,
    cot_s,
    cot_r,
    act_s,
    act_r,
    grd_s,
    grd_r,
    ghalo_s,
    ghalo_r,
    rsa_s,
    rsa_r,
    rsb_s,
    rsb_r,
    ya_s,
    ya_r,
    yb_s,
    yb_r,
    za_s,
    za_r,
    zb_s,
    zb_r,
    aga_s,
    aga_r,
    agb_s,
    agb_r,
):
    nbus, nx, ny, nz, scale = sizes
    rows, steps, chans = feat.shape
    block = rows // 2
    share = rows // nx
    nq = nx * CORES
    bus = lax.axis_index("bus")
    tm = lax.axis_index("tm")
    core = lax.rem(bus, CORES)
    yy = lax.rem(bus // CORES, ny)
    zz = bus // (CORES * ny)
    qq = tm * CORES + core

    def dev_bus(step):
        return {"bus": lax.rem(bus + (nbus + step), nbus), "tm": tm}

    def dev_x(step):
        return {"bus": bus, "tm": lax.rem(tm + step, nx)}

    def q_at(step):
        return lax.rem(qq + step, nq)

    def dev_q(step):
        other = q_at(step)
        return {"bus": bus - core + lax.rem(other, CORES), "tm": other // CORES}

    def dev_y(step):
        return {"bus": (zz * ny + lax.rem(yy + step, ny)) * CORES + core, "tm": tm}

    def dev_z(step):
        return {"bus": (lax.rem(zz + step, nz) * ny + yy) * CORES + core, "tm": tm}

    def remote(src, dst, send, recv, device):
        return pltpu.make_async_remote_copy(
            src_ref=src, dst_ref=dst, send_sem=send, recv_sem=recv, device_id=device, device_id_type=MESH
        )

    copy_feat = pltpu.make_async_copy(feat, fx.at[pl.ds(block, rows)], loc_sem.at[0])
    copy_cot = pltpu.make_async_copy(cot, cot_v, loc_sem.at[1])
    copy_own = pltpu.make_async_copy(cot.at[pl.ds(tm * share, share)], cot_w.at[tm], loc_sem.at[2])
    copy_feat.start()
    copy_own.start()
    copy_cot.start()

    partners = [dev_bus(-1), dev_bus(1)]
    partners += [dev_q(d) for d in range(1, nq)]
    partners += [dev_y(d) for d in range(1, ny)]
    partners += [dev_z(d) for d in range(1, nz)]
    barrier = pltpu.get_barrier_semaphore()
    for partner in partners:
        pl.semaphore_signal(barrier, inc=1, device_id=partner, device_id_type=MESH)

    side = 16 * steps
    row_id = lax.broadcasted_iota(jnp.int32, (side, side), 0)
    col_id = lax.broadcasted_iota(jnp.int32, (side, side), 1)
    swapped = (row_id % 16) * 16 + row_id // 16
    perm[...] = jnp.where(col_id == swapped, 1.0, 0.0).astype(BF16)

    for i in range(2):
        sums = [jnp.zeros((block, block), F32) for _ in range(4)]
        for k in range(8):
            target = nbr[i, k] - (2 * bus - 1)
            value = coup[i, k].astype(F32)
            for place in range(4):
                weight = jnp.where(target == place, 1.0, 0.0).astype(F32)
                sums[place] = sums[place] + weight * value
        full = jnp.concatenate(sums, axis=1)
        high, low = split(full)
        m_mat[0, pl.ds(i * block, block), :] = high
        m_mat[1, pl.ds(i * block, block), :] = low
    for part in range(2):
        mt_mat[part] = m_mat[part].astype(F32).T.astype(BF16)
    tap_rows = taps[...]
    spectrum = mm(fwd_tab[...], jnp.concatenate([tap_rows, tap_rows], axis=0))
    length = tap_rows.shape[0]
    kr[...] = spectrum[:length]
    ki[...] = spectrum[length:]

    pl.semaphore_wait(barrier, len(partners))

    to_next = remote(feat.at[pl.ds(block, block)], fx.at[pl.ds(0, block)], halo_s.at[0], halo_r.at[0], dev_bus(1))
    to_prev = remote(feat.at[pl.ds(0, block)], fx.at[pl.ds(rows + block, block)], halo_s.at[1], halo_r.at[1], dev_bus(-1))
    to_next.start()
    to_prev.start()
    cot_copies = []
    for d in range(1, nx):
        peer = lax.rem(tm + d, nx)
        cot_copies.append(
            remote(cot.at[pl.ds(peer * share, share)], cot_w.at[tm], cot_s.at[d], cot_r.at[d], dev_x(d))
        )
    for copy in cot_copies:
        copy.start()

    def to_time_major(src, dst, first, pairs):
        def body(pair, carry):
            at = first + pair * 32
            left = src[pl.ds(at, 16)].reshape(side, chans)
            right = src[pl.ds(at + 16, 16)].reshape(side, chans)
            moved = mm(perm[...], jnp.concatenate([left, right], axis=1)).astype(BF16)
            start = pl.multiple_of(at, 16)
            dst[:, pl.ds(start, 16), :] = moved[:, :chans].reshape(steps, 16, chans)
            dst[:, pl.ds(start + 16, 16), :] = moved[:, chans:].reshape(steps, 16, chans)
            return carry

        lax.fori_loop(0, pairs, body, 0)

    copy_feat.wait()
    to_time_major(fx, ft, block, rows // 32)
    to_next.wait()
    to_time_major(fx, ft, 0, block // 32)
    to_prev.wait()
    to_time_major(fx, ft, rows + block, block // 32)

    def forward(pair, carry):
        t = pair * 2
        both = jnp.concatenate([ft[t], ft[t + 1]], axis=1)
        mix = (mm(m_mat[0], both) + mm(m_mat[1], both)).astype(BF16)
        for half in range(2):
            mix_one = mix[:, half * chans : (half + 1) * chans]
            mixed[t + half] = mix_one
            pre = mm(mix_one, wg[...])
            gate = 1.0 / (1.0 + jnp.exp(-pre))
            act_t[t + half] = (pre * gate).astype(BF16)
            slope[t + half] = gate * (1.0 + pre * (1.0 - gate))
        return carry

    lax.fori_loop(0, steps // 2, forward, 0)

    def act_rows(at):
        start = pl.multiple_of(at, 16)
        left = act_t[:, pl.ds(start, 16), :].reshape(side, chans)
        right = act_t[:, pl.ds(start + 16, 16), :].reshape(side, chans)
        moved = mm(perm[...], jnp.concatenate([left, right], axis=1)).astype(BF16)
        return moved[:, :chans].reshape(16, steps, chans), moved[:, chans:].reshape(16, steps, chans)

    act_copies = []
    for d in list(range(1, nx)) + [0]:
        peer = lax.rem(tm + d, nx)
        for piece in range(share // 32):
            at = peer * share + piece * 32
            left, right = act_rows(at)
            if d == 0:
                act_w[tm, pl.ds(piece * 32, 16)] = left
                act_w[tm, pl.ds(piece * 32 + 16, 16)] = right
            else:
                act_b[d, pl.ds(piece * 32, 16)] = left
                act_b[d, pl.ds(piece * 32 + 16, 16)] = right
        if d:
            copy = remote(act_b.at[d], act_w.at[tm], act_s.at[d], act_r.at[d], dev_x(d))
            copy.start()
            act_copies.append(copy)

    copy_own.wait()
    for copy in cot_copies:
        copy.wait()

    group = 4
    lanes = group * chans

    def wide(src, at):
        cols = []
        for b in range(group):
            cols.append(jnp.concatenate([src[j, at + b] for j in range(nx)], axis=0))
        return jnp.concatenate(cols, axis=1)

    def tiled(table):
        return jnp.concatenate([table] * group, axis=1)

    def inverse(real, imag):
        high, low = split(jnp.concatenate([real, imag], axis=0))
        return mm(inv_tab[...], jnp.concatenate([high, low, high], axis=0))

    def backward(step, carry):
        at = step * group
        for j in range(nx):
            cot_rows = cot_w[j, pl.ds(at, group)].reshape(group * steps, chans)
            conv_rows = mm_t(cot_rows, wo[...], 1, 1).astype(BF16)
            gc_w[j] = conv_rows.reshape(group, steps, chans)
        data = wide(gc_w, 0)
        spec = mm(fwd_tab[...], jnp.concatenate([data, data], axis=0))
        g_freq[step] = spec
        gr, gi = spec[:length], spec[length:]
        k_re, k_im = tiled(kr[...]), tiled(ki[...])
        back = inverse(k_re * gr + k_im * gi, k_re * gi - k_im * gr).astype(BF16)
        for b in range(group):
            for j in range(nx):
                grad_w[j, at + b] = back[j * steps : (j + 1) * steps, b * chans : (b + 1) * chans]
        return carry

    lax.fori_loop(0, share // group, backward, 0)

    grad_copies = []
    for d in range(1, nx):
        peer = lax.rem(tm + d, nx)
        copy = remote(grad_w.at[peer], grad_b.at[pl.ds(tm * share, share)], grd_s.at[d], grd_r.at[d], dev_x(d))
        copy.start()
        grad_copies.append(copy)
    grad_b[pl.ds(tm * share, share)] = grad_w[tm]

    for copy in act_copies:
        copy.wait()

    red_b[...] = jnp.zeros_like(red_b)

    def convolve(step, carry):
        tap_re, tap_im = carry
        at = step * group
        data = wide(act_w, at)
        spec = mm(fwd_tab[...], jnp.concatenate([data, data], axis=0))
        ar, ai = spec[:length], spec[length:]
        k_re, k_im = tiled(kr[...]), tiled(ki[...])
        conv = inverse(k_re * ar - k_im * ai, k_re * ai + k_im * ar).astype(BF16)
        conv_rows = jnp.concatenate([conv[:, b * chans : (b + 1) * chans] for b in range(group)], axis=0)
        cot_cols = wide(cot_w, at)
        cot_rows = jnp.concatenate([cot_cols[:, b * chans : (b + 1) * chans] for b in range(group)], axis=0)
        red_b[pl.ds(0, chans), :] += mm_t(conv_rows, cot_rows, 0, 0)
        gr, gi = g_freq[step, pl.ds(0, length), :], g_freq[step, pl.ds(length, length), :]
        p_re = ar * gr + ai * gi
        p_im = ar * gi - ai * gr
        for b in range(group):
            tap_re = tap_re + p_re[:, b * chans : (b + 1) * chans]
            tap_im = tap_im + p_im[:, b * chans : (b + 1) * chans]
        return tap_re, tap_im

    zero = jnp.zeros((length, chans), F32)
    tap_re, tap_im = lax.fori_loop(0, share // group, convolve, (zero, zero))
    red_b[pl.ds(chans, length), :] = inverse(tap_re, tap_im)

    def scatter(red, rs, send, recv):
        size = red.shape[0] // nq
        copies = []
        for d in range(1, nq):
            start = pl.multiple_of(q_at(d) * size, 8)
            copy = remote(red.at[pl.ds(start, size)], rs.at[d], send.at[d], recv.at[d], dev_q(d))
            copy.start()
            copies.append(copy)
        return copies

    def exchange_y(red, rs, copies, buf, send, recv):
        size = red.shape[0] // nq
        for copy in copies:
            copy.wait()
        start = pl.multiple_of(qq * size, 8)
        total = red[pl.ds(start, size), :]
        for d in range(1, nq):
            total = total + rs[d]
        buf[yy] = total
        out = [remote(buf.at[yy], buf.at[yy], send.at[d], recv.at[d], dev_y(d)) for d in range(1, ny)]
        for copy in out:
            copy.start()
        return out

    def exchange_z(last, copies, buf, send, recv):
        for copy in copies:
            copy.wait()
        total = last[0]
        for i in range(1, ny):
            total = total + last[i]
        buf[zz] = total
        out = [remote(buf.at[zz], buf.at[zz], send.at[d], recv.at[d], dev_z(d)) for d in range(1, nz)]
        for copy in out:
            copy.start()
        return out

    def gather(red, last, copies, send, recv):
        size = red.shape[0] // nq
        for copy in copies:
            copy.wait()
        total = last[0]
        for i in range(1, nz):
            total = total + last[i]
        start = pl.multiple_of(qq * size, 8)
        red[pl.ds(start, size), :] = total
        piece = red.at[pl.ds(start, size)]
        out = [remote(piece, piece, send.at[d], recv.at[d], dev_q(d)) for d in range(1, nq)]
        for copy in out:
            copy.start()
        return out

    rs_b_copies = scatter(red_b, rs_b, rsb_s, rsb_r)

    for copy in grad_copies:
        copy.wait()
    to_time_major(grad_b, act_t, 0, rows // 32)
    red_a[...] = jnp.zeros_like(red_a)

    def graph_back(pair, carry):
        t = pair * 2
        rows_two = act_t[pl.ds(t, 2)].reshape(2 * rows, chans).astype(F32)
        slope_two = slope[pl.ds(t, 2)].reshape(2 * rows, chans)
        grad_pre = (rows_two * slope_two).astype(BF16)
        mixed_two = mixed[pl.ds(t, 2)].reshape(2 * rows, chans)
        red_a[...] += mm_t(mixed_two, grad_pre, 0, 0)
        grad_mixed = mm_t(grad_pre, wg[...], 1, 1).astype(BF16)
        both = jnp.concatenate([grad_mixed[:rows], grad_mixed[rows:]], axis=1)
        spread = mm(mt_mat[0], both) + mm(mt_mat[1], both)
        for half in range(2):
            part = spread[:, half * chans : (half + 1) * chans]
            send_prev[t + half] = part[:block].astype(BF16)
            own[t + half] = part[block : block + rows]
            send_next[t + half] = part[block + rows :].astype(BF16)
        return carry

    lax.fori_loop(0, steps // 2, graph_back, 0)
    grad_next = remote(send_next, from_prev, ghalo_s.at[0], ghalo_r.at[0], dev_bus(1))
    grad_prev = remote(send_prev, from_next, ghalo_s.at[1], ghalo_r.at[1], dev_bus(-1))
    grad_next.start()
    grad_prev.start()
    rs_a_copies = scatter(red_a, rs_a, rsa_s, rsa_r)
    y_b_copies = exchange_y(red_b, rs_b, rs_b_copies, y_b, yb_s, yb_r)
    y_a_copies = exchange_y(red_a, rs_a, rs_a_copies, y_a, ya_s, ya_r)
    z_b_copies = exchange_z(y_b, y_b_copies, z_b, zb_s, zb_r)
    z_a_copies = exchange_z(y_a, y_a_copies, z_a, za_s, za_r)

    grad_next.wait()
    grad_prev.wait()
    copy_cot.wait()

    def finish(piece, carry):
        at = pl.multiple_of(piece * 16, 16)
        for half, other in ((0, from_prev), (1, from_next)):
            first = pl.multiple_of(half * block + at, 16)
            total = own[:, pl.ds(first, 16), :] + other[:, pl.ds(at, 16), :].astype(F32)
            high, low = split(total.reshape(side, chans))
            both = mm(perm[...], jnp.concatenate([high, low], axis=1))
            moved = both[:, :chans] + both[:, chans:]
            base = cot_v[pl.ds(first, 16)].reshape(side, chans).astype(F32)
            out_v[pl.ds(first, 16)] = (moved + base).astype(BF16).reshape(16, steps, chans)
        return carry

    lax.fori_loop(0, block // 16, finish, 0)
    copy_out = pltpu.make_async_copy(out_v, grad_feat, out_sem)
    copy_out.start()

    ag_b_copies = gather(sum_b, z_b, z_b_copies, agb_s, agb_r)
    ag_a_copies = gather(sum_a, z_a, z_a_copies, aga_s, aga_r)
    for copy in ag_b_copies:
        copy.wait()
    grad_out[...] = sum_b[pl.ds(0, chans), :] * scale
    grad_taps[...] = sum_b[pl.ds(chans, length), :] * scale
    for copy in ag_a_copies:
        copy.wait()
    grad_graph[...] = sum_a[...] * scale
    copy_out.wait()


def shards(sizes, features, couplings, neighbors, w_graph, kernel_taps, w_out, cotangent):
    nbus, nx, ny, nz, scale = sizes
    rows, steps, chans = features.shape
    length = kernel_taps.shape[0]
    block = couplings.shape[2]
    share = rows // nx
    nq = nx * CORES
    group = 4
    fwd_tab, inv_tab = dft_tables(length)
    size_a = chans // nq
    size_b = (chans + length) // nq
    vmem = pltpu.VMEM
    dma = pltpu.SemaphoreType.DMA
    in_vmem = pl.BlockSpec(memory_space=pltpu.VMEM)
    in_any = pl.BlockSpec(memory_space=pl.ANY)
    scratch = [
        vmem((rows + 2 * block, steps, chans), BF16),
        vmem((steps, rows + 2 * block, chans), BF16),
        vmem((16 * steps, 16 * steps), BF16),
        vmem((2, rows, rows + 2 * block), BF16),
        vmem((2, rows + 2 * block, rows), BF16),
        vmem((steps, rows, chans), BF16),
        vmem((steps, rows, chans), F32),
        vmem((steps, rows, chans), BF16),
        vmem((nx, share, steps, chans), BF16),
        vmem((nx, share, steps, chans), BF16),
        vmem((rows, steps, chans), BF16),
        vmem((nx, share, steps, chans), BF16),
        vmem((nx, group, steps, chans), BF16),
        vmem((share // group, 2 * length, group * chans), F32),
        vmem((length, chans), F32),
        vmem((length, chans), F32),
        vmem((nx, share, steps, chans), BF16),
        vmem((rows, steps, chans), BF16),
        vmem((steps, rows, chans), F32),
        vmem((steps, block, chans), BF16),
        vmem((steps, block, chans), BF16),
        vmem((steps, block, chans), BF16),
        vmem((steps, block, chans), BF16),
        vmem((rows, steps, chans), BF16),
        vmem((chans, chans), F32),
        vmem((nq, size_a, chans), F32),
        vmem((ny, size_a, chans), F32),
        vmem((nz, size_a, chans), F32),
        vmem((chans, chans), F32),
        vmem((chans + length, chans), F32),
        vmem((nq, size_b, chans), F32),
        vmem((ny, size_b, chans), F32),
        vmem((nz, size_b, chans), F32),
        vmem((chans + length, chans), F32),
        dma((3,)),
        dma,
    ]
    for count in (2, nx, nx, nx, 2, nq, nq, ny, ny, nz, nz, nq, nq):
        scratch += [dma((count,)), dma((count,))]
    return pl.pallas_call(
        functools.partial(kernel, sizes),
        out_shape=(
            jax.ShapeDtypeStruct(features.shape, BF16),
            jax.ShapeDtypeStruct((chans, chans), F32),
            jax.ShapeDtypeStruct((chans, chans), F32),
            jax.ShapeDtypeStruct((length, chans), F32),
        ),
        in_specs=[in_any, in_any, in_vmem, pl.BlockSpec(memory_space=pltpu.SMEM)] + [in_vmem] * 5,
        out_specs=(in_any, in_vmem, in_vmem, in_vmem),
        scratch_shapes=scratch,
        compiler_params=pltpu.CompilerParams(
            collective_id=0, has_side_effects=True, vmem_limit_bytes=40 * 1024 * 1024
        ),
    )(features, cotangent, couplings, neighbors, w_graph, kernel_taps, w_out, jnp.asarray(fwd_tab), jnp.asarray(inv_tab))


def solution(mesh):
    nbus, nx = mesh.shape["bus"], mesh.shape["tm"]
    nz = nbus // (CORES * CHIPS_Y)

    def step(features, couplings, neighbors, w_graph, kernel_taps, w_out, cotangent):
        total_rows = nbus * features.shape[0] * features.shape[1] * nx
        sizes = (nbus, nx, CHIPS_Y, nz, 1.0 / math.sqrt(total_rows))
        return shards(sizes, features, couplings, neighbors, w_graph, kernel_taps, w_out, cotangent)

    return jax.shard_map(
        step,
        mesh=mesh,
        in_specs=(
            P("bus", "tm", None),
            P("bus", None, None, None),
            P("bus", None),
            P(),
            P(),
            P(),
            P("bus", "tm", None),
        ),
        out_specs=(P("bus", "tm", None), P(), P(), P()),
        check_vma=False,
    )
```

```python
import functools
import math

import jax
import jax.numpy as jnp
import ml_dtypes
import numpy as np
from jax import lax
from jax.experimental import pallas as pl
from jax.experimental.pallas import tpu as pltpu
from jax.sharding import PartitionSpec as P

CORES = 2
CHIPS_Y = 4
MESH = pl.DeviceIdType.MESH
F32 = jnp.float32
BF16 = jnp.bfloat16


def dft_tables(length):
    freq = 2 * np.arange(length)[:, None] + 1
    angle = np.pi * freq * np.arange(length)[None, :] / (2 * length)
    forward = np.concatenate([np.cos(angle), -np.sin(angle)], axis=0)
    inverse = forward.T / length

    def parts(table):
        high = table.astype(ml_dtypes.bfloat16)
        low = (table - high.astype(np.float64)).astype(ml_dtypes.bfloat16)
        return high, low

    f_high, f_low = parts(forward)
    i_high, i_low = parts(inverse)
    return (
        np.concatenate([f_high, f_low], axis=1),
        np.concatenate([i_high, i_high, i_low], axis=1),
    )


def split(value):
    high = value.astype(BF16)
    low = (value - high.astype(F32)).astype(BF16)
    return high, low


def mm(a, b):
    return jnp.dot(a, b, preferred_element_type=F32)


def mm_t(a, b, da, db):
    return lax.dot_general(a, b, (((da,), (db,)), ((), ())), preferred_element_type=F32)


def kernel(
    sizes,
    feat,
    cot,
    coup_h,
    nbr_h,
    wg_h,
    taps_h,
    wo_h,
    fwd_h,
    inv_h,
    grad_feat,
    grad_graph,
    grad_out,
    grad_taps,
    coup,
    nbr,
    wg,
    taps,
    wo,
    fwd_tab,
    inv_tab,
    fx,
    ft,
    perm,
    m_mat,
    mt_mat,
    mixed,
    slope,
    act_t,
    act_b,
    act_w,
    cot_v,
    cot_w,
    gc_w,
    g_freq,
    kr,
    ki,
    grad_w,
    grad_b,
    own,
    send_prev,
    send_next,
    from_prev,
    from_next,
    red_a,
    rs_a,
    y_a,
    z_a,
    sum_a,
    red_b,
    rs_b,
    y_b,
    z_b,
    sum_b,
    loc_sem,
    halo_s,
    halo_r,
    cot_s,
    cot_r,
    act_s,
    act_r,
    grd_s,
    grd_r,
    ghalo_s,
    ghalo_r,
    rsa_s,
    rsa_r,
    rsb_s,
    rsb_r,
    ya_s,
    ya_r,
    yb_s,
    yb_r,
    za_s,
    za_r,
    zb_s,
    zb_r,
    aga_s,
    aga_r,
    agb_s,
    agb_r,
):
    nbus, nx, ny, nz, scale = sizes
    rows, steps, chans = feat.shape
    block = rows // 2
    share = rows // nx
    nq = nx * CORES
    bus = lax.axis_index("bus")
    tm = lax.axis_index("tm")
    core = lax.rem(bus, CORES)
    yy = lax.rem(bus // CORES, ny)
    zz = bus // (CORES * ny)
    qq = tm * CORES + core

    def dev_bus(step):
        return {"bus": lax.rem(bus + (nbus + step), nbus), "tm": tm}

    def dev_x(step):
        return {"bus": bus, "tm": lax.rem(tm + step, nx)}

    def q_at(step):
        return lax.rem(qq + step, nq)

    def dev_q(step):
        other = q_at(step)
        return {"bus": bus - core + lax.rem(other, CORES), "tm": other // CORES}

    def dev_y(step):
        return {"bus": (zz * ny + lax.rem(yy + step, ny)) * CORES + core, "tm": tm}

    def dev_z(step):
        return {"bus": (lax.rem(zz + step, nz) * ny + yy) * CORES + core, "tm": tm}

    def remote(src, dst, send, recv, device):
        return pltpu.make_async_remote_copy(
            src_ref=src, dst_ref=dst, send_sem=send, recv_sem=recv, device_id=device, device_id_type=MESH
        )

    copy_feat = pltpu.make_async_copy(feat, fx.at[pl.ds(block, rows)], loc_sem.at[0])
    copy_cot = pltpu.make_async_copy(cot, cot_v, loc_sem.at[1])
    copy_own = pltpu.make_async_copy(cot.at[pl.ds(tm * share, share)], cot_w.at[tm], loc_sem.at[2])
    small = [(nbr_h, nbr), (coup_h, coup), (taps_h, taps), (fwd_h, fwd_tab), (wg_h, wg), (wo_h, wo), (inv_h, inv_tab)]
    small_copies = [pltpu.make_async_copy(src, dst, loc_sem.at[3 + i]) for i, (src, dst) in enumerate(small)]
    for copy in small_copies:
        copy.start()
    copy_feat.start()
    copy_own.start()
    copy_cot.start()

    partners = [dev_bus(-1), dev_bus(1)]
    partners += [dev_q(d) for d in range(1, nq)]
    partners += [dev_y(d) for d in range(1, ny)]
    partners += [dev_z(d) for d in range(1, nz)]
    barrier = pltpu.get_barrier_semaphore()
    for partner in partners:
        pl.semaphore_signal(barrier, inc=1, device_id=partner, device_id_type=MESH)

    side = 16 * steps
    row_id = lax.broadcasted_iota(jnp.int32, (side, side), 0)
    col_id = lax.broadcasted_iota(jnp.int32, (side, side), 1)
    swapped = (row_id % 16) * 16 + row_id // 16
    perm[...] = jnp.where(col_id == swapped, 1.0, 0.0).astype(BF16)

    for copy in small_copies:
        copy.wait()
    for i in range(2):
        sums = [jnp.zeros((block, block), F32) for _ in range(4)]
        for k in range(8):
            target = nbr[i, k] - (2 * bus - 1)
            value = coup[i, k].astype(F32)
            for place in range(4):
                weight = jnp.where(target == place, 1.0, 0.0).astype(F32)
                sums[place] = sums[place] + weight * value
        full = jnp.concatenate(sums, axis=1)
        high, low = split(full)
        m_mat[0, pl.ds(i * block, block), :] = high
        m_mat[1, pl.ds(i * block, block), :] = low
    for part in range(2):
        mt_mat[part] = m_mat[part].astype(F32).T.astype(BF16)
    tap_rows = taps[...]
    spectrum = mm(fwd_tab[...], jnp.concatenate([tap_rows, tap_rows], axis=0))
    length = tap_rows.shape[0]
    kr[...] = spectrum[:length]
    ki[...] = spectrum[length:]

    pl.semaphore_wait(barrier, len(partners))

    to_next = remote(feat.at[pl.ds(block, block)], fx.at[pl.ds(0, block)], halo_s.at[0], halo_r.at[0], dev_bus(1))
    to_prev = remote(feat.at[pl.ds(0, block)], fx.at[pl.ds(rows + block, block)], halo_s.at[1], halo_r.at[1], dev_bus(-1))
    to_next.start()
    to_prev.start()
    cot_copies = []
    for d in range(1, nx):
        peer = lax.rem(tm + d, nx)
        cot_copies.append(
            remote(cot.at[pl.ds(peer * share, share)], cot_w.at[tm], cot_s.at[d], cot_r.at[d], dev_x(d))
        )
    for copy in cot_copies:
        copy.start()

    def to_time_major(src, dst, first, pairs):
        def body(pair, carry):
            at = first + pair * 32
            left = src[pl.ds(at, 16)].reshape(side, chans)
            right = src[pl.ds(at + 16, 16)].reshape(side, chans)
            moved = mm(perm[...], jnp.concatenate([left, right], axis=1)).astype(BF16)
            start = pl.multiple_of(at, 16)
            dst[:, pl.ds(start, 16), :] = moved[:, :chans].reshape(steps, 16, chans)
            dst[:, pl.ds(start + 16, 16), :] = moved[:, chans:].reshape(steps, 16, chans)
            return carry

        lax.fori_loop(0, pairs, body, 0)

    copy_feat.wait()
    to_time_major(fx, ft, block, rows // 32)
    to_next.wait()
    to_time_major(fx, ft, 0, block // 32)
    to_prev.wait()
    to_time_major(fx, ft, rows + block, block // 32)

    def forward(pair, carry):
        t = pair * 2
        both = jnp.concatenate([ft[t], ft[t + 1]], axis=1)
        mix = (mm(m_mat[0], both) + mm(m_mat[1], both)).astype(BF16)
        for half in range(2):
            mix_one = mix[:, half * chans : (half + 1) * chans]
            mixed[t + half] = mix_one
            pre = mm(mix_one, wg[...])
            gate = 1.0 / (1.0 + jnp.exp(-pre))
            act_t[t + half] = (pre * gate).astype(BF16)
            slope[t + half] = gate * (1.0 + pre * (1.0 - gate))
        return carry

    lax.fori_loop(0, steps // 2, forward, 0)

    def act_rows(at):
        start = pl.multiple_of(at, 16)
        left = act_t[:, pl.ds(start, 16), :].reshape(side, chans)
        right = act_t[:, pl.ds(start + 16, 16), :].reshape(side, chans)
        moved = mm(perm[...], jnp.concatenate([left, right], axis=1)).astype(BF16)
        return moved[:, :chans].reshape(16, steps, chans), moved[:, chans:].reshape(16, steps, chans)

    act_copies = []
    for d in list(range(1, nx)) + [0]:
        peer = lax.rem(tm + d, nx)
        for piece in range(share // 32):
            at = peer * share + piece * 32
            left, right = act_rows(at)
            if d == 0:
                act_w[tm, pl.ds(piece * 32, 16)] = left
                act_w[tm, pl.ds(piece * 32 + 16, 16)] = right
            else:
                act_b[d, pl.ds(piece * 32, 16)] = left
                act_b[d, pl.ds(piece * 32 + 16, 16)] = right
        if d:
            copy = remote(act_b.at[d], act_w.at[tm], act_s.at[d], act_r.at[d], dev_x(d))
            copy.start()
            act_copies.append(copy)

    copy_own.wait()
    for copy in cot_copies:
        copy.wait()

    group = 4
    lanes = group * chans

    def wide(src, at):
        cols = []
        for b in range(group):
            cols.append(jnp.concatenate([src[j, at + b] for j in range(nx)], axis=0))
        return jnp.concatenate(cols, axis=1)

    def tiled(table):
        return jnp.concatenate([table] * group, axis=1)

    def inverse(real, imag):
        high, low = split(jnp.concatenate([real, imag], axis=0))
        return mm(inv_tab[...], jnp.concatenate([high, low, high], axis=0))

    def backward(step, carry):
        at = step * group
        for j in range(nx):
            cot_rows = cot_w[j, pl.ds(at, group)].reshape(group * steps, chans)
            conv_rows = mm_t(cot_rows, wo[...], 1, 1).astype(BF16)
            gc_w[j] = conv_rows.reshape(group, steps, chans)
        data = wide(gc_w, 0)
        spec = mm(fwd_tab[...], jnp.concatenate([data, data], axis=0))
        g_freq[step] = spec
        gr, gi = spec[:length], spec[length:]
        k_re, k_im = tiled(kr[...]), tiled(ki[...])
        back = inverse(k_re * gr + k_im * gi, k_re * gi - k_im * gr).astype(BF16)
        for b in range(group):
            for j in range(nx):
                grad_w[j, at + b] = back[j * steps : (j + 1) * steps, b * chans : (b + 1) * chans]
        return carry

    lax.fori_loop(0, share // group, backward, 0)

    grad_copies = []
    for d in range(1, nx):
        peer = lax.rem(tm + d, nx)
        copy = remote(grad_w.at[peer], grad_b.at[pl.ds(tm * share, share)], grd_s.at[d], grd_r.at[d], dev_x(d))
        copy.start()
        grad_copies.append(copy)
    grad_b[pl.ds(tm * share, share)] = grad_w[tm]

    for copy in act_copies:
        copy.wait()

    red_b[...] = jnp.zeros_like(red_b)

    def convolve(step, carry):
        tap_re, tap_im = carry
        at = step * group
        data = wide(act_w, at)
        spec = mm(fwd_tab[...], jnp.concatenate([data, data], axis=0))
        ar, ai = spec[:length], spec[length:]
        k_re, k_im = tiled(kr[...]), tiled(ki[...])
        conv = inverse(k_re * ar - k_im * ai, k_re * ai + k_im * ar).astype(BF16)
        conv_rows = jnp.concatenate([conv[:, b * chans : (b + 1) * chans] for b in range(group)], axis=0)
        cot_cols = wide(cot_w, at)
        cot_rows = jnp.concatenate([cot_cols[:, b * chans : (b + 1) * chans] for b in range(group)], axis=0)
        red_b[pl.ds(0, chans), :] += mm_t(conv_rows, cot_rows, 0, 0)
        gr, gi = g_freq[step, pl.ds(0, length), :], g_freq[step, pl.ds(length, length), :]
        p_re = ar * gr + ai * gi
        p_im = ar * gi - ai * gr
        for b in range(group):
            tap_re = tap_re + p_re[:, b * chans : (b + 1) * chans]
            tap_im = tap_im + p_im[:, b * chans : (b + 1) * chans]
        return tap_re, tap_im

    zero = jnp.zeros((length, chans), F32)
    tap_re, tap_im = lax.fori_loop(0, share // group, convolve, (zero, zero))
    red_b[pl.ds(chans, length), :] = inverse(tap_re, tap_im)

    def scatter(red, rs, send, recv):
        size = red.shape[0] // nq
        copies = []
        for d in range(1, nq):
            start = pl.multiple_of(q_at(d) * size, 8)
            copy = remote(red.at[pl.ds(start, size)], rs.at[d], send.at[d], recv.at[d], dev_q(d))
            copy.start()
            copies.append(copy)
        return copies

    def exchange_y(red, rs, copies, buf, send, recv):
        size = red.shape[0] // nq
        for copy in copies:
            copy.wait()
        start = pl.multiple_of(qq * size, 8)
        total = red[pl.ds(start, size), :]
        for d in range(1, nq):
            total = total + rs[d]
        buf[yy] = total
        out = [remote(buf.at[yy], buf.at[yy], send.at[d], recv.at[d], dev_y(d)) for d in range(1, ny)]
        for copy in out:
            copy.start()
        return out

    def exchange_z(last, copies, buf, send, recv):
        for copy in copies:
            copy.wait()
        total = last[0]
        for i in range(1, ny):
            total = total + last[i]
        buf[zz] = total
        out = [remote(buf.at[zz], buf.at[zz], send.at[d], recv.at[d], dev_z(d)) for d in range(1, nz)]
        for copy in out:
            copy.start()
        return out

    def gather(red, last, copies, send, recv):
        size = red.shape[0] // nq
        for copy in copies:
            copy.wait()
        total = last[0]
        for i in range(1, nz):
            total = total + last[i]
        start = pl.multiple_of(qq * size, 8)
        red[pl.ds(start, size), :] = total
        piece = red.at[pl.ds(start, size)]
        out = [remote(piece, piece, send.at[d], recv.at[d], dev_q(d)) for d in range(1, nq)]
        for copy in out:
            copy.start()
        return out

    rs_b_copies = scatter(red_b, rs_b, rsb_s, rsb_r)

    for copy in grad_copies:
        copy.wait()
    to_time_major(grad_b, act_t, 0, rows // 32)
    red_a[...] = jnp.zeros_like(red_a)

    def graph_back(pair, carry):
        t = pair * 2
        rows_two = act_t[pl.ds(t, 2)].reshape(2 * rows, chans).astype(F32)
        slope_two = slope[pl.ds(t, 2)].reshape(2 * rows, chans)
        grad_pre = (rows_two * slope_two).astype(BF16)
        mixed_two = mixed[pl.ds(t, 2)].reshape(2 * rows, chans)
        red_a[...] += mm_t(mixed_two, grad_pre, 0, 0)
        grad_mixed = mm_t(grad_pre, wg[...], 1, 1).astype(BF16)
        both = jnp.concatenate([grad_mixed[:rows], grad_mixed[rows:]], axis=1)
        spread = mm(mt_mat[0], both) + mm(mt_mat[1], both)
        for half in range(2):
            part = spread[:, half * chans : (half + 1) * chans]
            send_prev[t + half] = part[:block].astype(BF16)
            own[t + half] = part[block : block + rows]
            send_next[t + half] = part[block + rows :].astype(BF16)
        return carry

    lax.fori_loop(0, steps // 2, graph_back, 0)
    grad_next = remote(send_next, from_prev, ghalo_s.at[0], ghalo_r.at[0], dev_bus(1))
    grad_prev = remote(send_prev, from_next, ghalo_s.at[1], ghalo_r.at[1], dev_bus(-1))
    grad_next.start()
    grad_prev.start()
    rs_a_copies = scatter(red_a, rs_a, rsa_s, rsa_r)
    y_b_copies = exchange_y(red_b, rs_b, rs_b_copies, y_b, yb_s, yb_r)
    y_a_copies = exchange_y(red_a, rs_a, rs_a_copies, y_a, ya_s, ya_r)
    z_b_copies = exchange_z(y_b, y_b_copies, z_b, zb_s, zb_r)
    z_a_copies = exchange_z(y_a, y_a_copies, z_a, za_s, za_r)

    grad_next.wait()
    grad_prev.wait()
    copy_cot.wait()

    def finish(piece, carry):
        at = pl.multiple_of(piece * 16, 16)
        for half, other in ((0, from_prev), (1, from_next)):
            first = pl.multiple_of(half * block + at, 16)
            total = own[:, pl.ds(first, 16), :] + other[:, pl.ds(at, 16), :].astype(F32)
            high, low = split(total.reshape(side, chans))
            both = mm(perm[...], jnp.concatenate([high, low], axis=1))
            moved = both[:, :chans] + both[:, chans:]
            base = cot_v[pl.ds(first, 16)].reshape(side, chans).astype(F32)
            grad_feat[pl.ds(first, 16)] = (moved + base).astype(BF16).reshape(16, steps, chans)
        return carry

    lax.fori_loop(0, block // 16, finish, 0)

    ag_b_copies = gather(sum_b, z_b, z_b_copies, agb_s, agb_r)
    ag_a_copies = gather(sum_a, z_a, z_a_copies, aga_s, aga_r)
    for copy in ag_b_copies:
        copy.wait()
    grad_out[...] = sum_b[pl.ds(0, chans), :] * scale
    grad_taps[...] = sum_b[pl.ds(chans, length), :] * scale
    for copy in ag_a_copies:
        copy.wait()
    grad_graph[...] = sum_a[...] * scale


def shards(sizes, features, couplings, neighbors, w_graph, kernel_taps, w_out, cotangent):
    nbus, nx, ny, nz, scale = sizes
    rows, steps, chans = features.shape
    length = kernel_taps.shape[0]
    block = couplings.shape[2]
    share = rows // nx
    nq = nx * CORES
    group = 4
    fwd_tab, inv_tab = dft_tables(length)
    size_a = chans // nq
    size_b = (chans + length) // nq
    vmem = pltpu.VMEM
    dma = pltpu.SemaphoreType.DMA
    in_vmem = pl.BlockSpec(memory_space=pltpu.VMEM)
    in_any = pl.BlockSpec(memory_space=pl.ANY)
    in_hbm = pl.BlockSpec(memory_space=pltpu.HBM)
    scratch = [
        vmem(couplings.shape, BF16),
        pltpu.SMEM(neighbors.shape, jnp.int32),
        vmem(w_graph.shape, BF16),
        vmem(kernel_taps.shape, BF16),
        vmem(w_out.shape, BF16),
        vmem(fwd_tab.shape, BF16),
        vmem(inv_tab.shape, BF16),
        vmem((rows + 2 * block, steps, chans), BF16),
        vmem((steps, rows + 2 * block, chans), BF16),
        vmem((16 * steps, 16 * steps), BF16),
        vmem((2, rows, rows + 2 * block), BF16),
        vmem((2, rows + 2 * block, rows), BF16),
        vmem((steps, rows, chans), BF16),
        vmem((steps, rows, chans), F32),
        vmem((steps, rows, chans), BF16),
        vmem((nx, share, steps, chans), BF16),
        vmem((nx, share, steps, chans), BF16),
        vmem((rows, steps, chans), BF16),
        vmem((nx, share, steps, chans), BF16),
        vmem((nx, group, steps, chans), BF16),
        vmem((share // group, 2 * length, group * chans), F32),
        vmem((length, chans), F32),
        vmem((length, chans), F32),
        vmem((nx, share, steps, chans), BF16),
        vmem((rows, steps, chans), BF16),
        vmem((steps, rows, chans), F32),
        vmem((steps, block, chans), BF16),
        vmem((steps, block, chans), BF16),
        vmem((steps, block, chans), BF16),
        vmem((steps, block, chans), BF16),
        vmem((chans, chans), F32),
        vmem((nq, size_a, chans), F32),
        vmem((ny, size_a, chans), F32),
        vmem((nz, size_a, chans), F32),
        vmem((chans, chans), F32),
        vmem((chans + length, chans), F32),
        vmem((nq, size_b, chans), F32),
        vmem((ny, size_b, chans), F32),
        vmem((nz, size_b, chans), F32),
        vmem((chans + length, chans), F32),
        dma((10,)),
    ]
    for count in (2, nx, nx, nx, 2, nq, nq, ny, ny, nz, nz, nq, nq):
        scratch += [dma((count,)), dma((count,))]
    return pl.pallas_call(
        functools.partial(kernel, sizes),
        out_shape=(
            jax.ShapeDtypeStruct(features.shape, BF16),
            jax.ShapeDtypeStruct((chans, chans), F32),
            jax.ShapeDtypeStruct((chans, chans), F32),
            jax.ShapeDtypeStruct((length, chans), F32),
        ),
        in_specs=[in_hbm] * 9,
        out_specs=(in_vmem, in_vmem, in_vmem, in_vmem),
        scratch_shapes=scratch,
        compiler_params=pltpu.CompilerParams(
            collective_id=0, has_side_effects=True, vmem_limit_bytes=67043328
        ),
    )(features, cotangent, couplings, neighbors, w_graph, kernel_taps, w_out, jnp.asarray(fwd_tab), jnp.asarray(inv_tab))


def solution(mesh):
    nbus, nx = mesh.shape["bus"], mesh.shape["tm"]
    nz = nbus // (CORES * CHIPS_Y)

    def step(features, couplings, neighbors, w_graph, kernel_taps, w_out, cotangent):
        total_rows = nbus * features.shape[0] * features.shape[1] * nx
        sizes = (nbus, nx, CHIPS_Y, nz, 1.0 / math.sqrt(total_rows))
        return shards(sizes, features, couplings, neighbors, w_graph, kernel_taps, w_out, cotangent)

    return jax.shard_map(
        step,
        mesh=mesh,
        in_specs=(
            P("bus", "tm", None),
            P("bus", None, None, None),
            P("bus", None),
            P(),
            P(),
            P(),
            P("bus", "tm", None),
        ),
        out_specs=(P("bus", "tm", None), P(), P(), P()),
        check_vma=False,
    )
```

```python
import functools
import math

import jax
import jax.numpy as jnp
import ml_dtypes
import numpy as np
from jax import lax
from jax.experimental import pallas as pl
from jax.experimental.pallas import tpu as pltpu
from jax.sharding import PartitionSpec as P

CORES = 2
CHIPS_Y = 4
MESH = pl.DeviceIdType.MESH
F32 = jnp.float32
BF16 = jnp.bfloat16


def dft_tables(length):
    freq = 2 * np.arange(length)[:, None] + 1
    angle = np.pi * freq * np.arange(length)[None, :] / (2 * length)
    forward = np.concatenate([np.cos(angle), -np.sin(angle)], axis=0)
    inverse = forward.T / length

    def parts(table):
        high = table.astype(ml_dtypes.bfloat16)
        low = (table - high.astype(np.float64)).astype(ml_dtypes.bfloat16)
        return high, low

    f_high, f_low = parts(forward)
    i_high, i_low = parts(inverse)
    return (
        np.concatenate([f_high, f_low], axis=1),
        np.concatenate([i_high, i_high, i_low], axis=1),
    )


def split(value):
    high = value.astype(BF16)
    low = (value - high.astype(F32)).astype(BF16)
    return high, low


def mm(a, b):
    return jnp.dot(a, b, preferred_element_type=F32)


def mm_t(a, b, da, db):
    return lax.dot_general(a, b, (((da,), (db,)), ((), ())), preferred_element_type=F32)


def kernel(
    sizes,
    feat,
    cot,
    coup_h,
    nbr_h,
    wg_h,
    taps_h,
    wo_h,
    fwd_h,
    inv_h,
    grad_feat,
    grad_graph,
    grad_out,
    grad_taps,
    coup,
    nbr,
    wg,
    taps,
    wo,
    fwd_tab,
    inv_tab,
    fx,
    ft,
    perm,
    m_mat,
    mt_mat,
    mixed,
    slope,
    act_t,
    act_b,
    act_w,
    cot_v,
    cot_w,
    gc_w,
    g_freq,
    kr,
    ki,
    grad_w,
    grad_b,
    own,
    send_prev,
    send_next,
    from_prev,
    from_next,
    red_a,
    rs_a,
    y_a,
    z_a,
    sum_a,
    red_b,
    rs_b,
    y_b,
    z_b,
    sum_b,
    loc_sem,
    halo_s,
    halo_r,
    cot_s,
    cot_r,
    act_s,
    act_r,
    grd_s,
    grd_r,
    ghalo_s,
    ghalo_r,
    rsa_s,
    rsa_r,
    rsb_s,
    rsb_r,
    ya_s,
    ya_r,
    yb_s,
    yb_r,
    za_s,
    za_r,
    zb_s,
    zb_r,
    aga_s,
    aga_r,
    agb_s,
    agb_r,
):
    nbus, nx, ny, nz, scale = sizes
    rows, steps, chans = feat.shape
    block = rows // 2
    share = rows // nx
    nq = nx * CORES
    bus = lax.axis_index("bus")
    tm = lax.axis_index("tm")
    core = lax.rem(bus, CORES)
    yy = lax.rem(bus // CORES, ny)
    zz = bus // (CORES * ny)
    qq = tm * CORES + core

    def dev_bus(step):
        return {"bus": lax.rem(bus + (nbus + step), nbus), "tm": tm}

    def dev_x(step):
        return {"bus": bus, "tm": lax.rem(tm + step, nx)}

    def q_at(step):
        return lax.rem(qq + step, nq)

    def dev_q(step):
        other = q_at(step)
        return {"bus": bus - core + lax.rem(other, CORES), "tm": other // CORES}

    def dev_y(step):
        return {"bus": (zz * ny + lax.rem(yy + step, ny)) * CORES + core, "tm": tm}

    def dev_z(step):
        return {"bus": (lax.rem(zz + step, nz) * ny + yy) * CORES + core, "tm": tm}

    def remote(src, dst, send, recv, device):
        return pltpu.make_async_remote_copy(
            src_ref=src, dst_ref=dst, send_sem=send, recv_sem=recv, device_id=device, device_id_type=MESH
        )

    copy_feat = pltpu.make_async_copy(feat, fx.at[pl.ds(block, rows)], loc_sem.at[0])
    copy_cot = pltpu.make_async_copy(cot, cot_v, loc_sem.at[1])
    copy_own = pltpu.make_async_copy(cot.at[pl.ds(tm * share, share)], cot_w.at[tm], loc_sem.at[2])
    small = [(nbr_h, nbr), (coup_h, coup), (taps_h, taps), (fwd_h, fwd_tab), (wg_h, wg), (wo_h, wo), (inv_h, inv_tab)]
    small_copies = [pltpu.make_async_copy(src, dst, loc_sem.at[3 + i]) for i, (src, dst) in enumerate(small)]
    for copy in small_copies:
        copy.start()
    copy_feat.start()
    copy_own.start()
    copy_cot.start()

    partners = [dev_bus(-1), dev_bus(1)]
    partners += [dev_q(d) for d in range(1, nq)]
    partners += [dev_y(d) for d in range(1, ny)]
    partners += [dev_z(d) for d in range(1, nz)]
    barrier = pltpu.get_barrier_semaphore()
    for partner in partners:
        pl.semaphore_signal(barrier, inc=1, device_id=partner, device_id_type=MESH)

    side = 16 * steps
    row_id = lax.broadcasted_iota(jnp.int32, (side, side), 0)
    col_id = lax.broadcasted_iota(jnp.int32, (side, side), 1)
    swapped = (row_id % 16) * 16 + row_id // 16
    perm[...] = jnp.where(col_id == swapped, 1.0, 0.0).astype(BF16)

    for copy in small_copies:
        copy.wait()
    for i in range(2):
        sums = [jnp.zeros((block, block), F32) for _ in range(4)]
        for k in range(8):
            target = nbr[i, k] - (2 * bus - 1)
            value = coup[i, k].astype(F32)
            for place in range(4):
                weight = jnp.where(target == place, 1.0, 0.0).astype(F32)
                sums[place] = sums[place] + weight * value
        full = jnp.concatenate(sums, axis=1)
        high, low = split(full)
        m_mat[0, pl.ds(i * block, block), :] = high
        m_mat[1, pl.ds(i * block, block), :] = low
    for part in range(2):
        mt_mat[part] = m_mat[part].astype(F32).T.astype(BF16)
    tap_rows = taps[...]
    spectrum = mm(fwd_tab[...], jnp.concatenate([tap_rows, tap_rows], axis=0))
    length = tap_rows.shape[0]
    kr[...] = spectrum[:length]
    ki[...] = spectrum[length:]

    pl.semaphore_wait(barrier, len(partners))

    to_next = remote(feat.at[pl.ds(block, block)], fx.at[pl.ds(0, block)], halo_s.at[0], halo_r.at[0], dev_bus(1))
    to_prev = remote(feat.at[pl.ds(0, block)], fx.at[pl.ds(rows + block, block)], halo_s.at[1], halo_r.at[1], dev_bus(-1))
    to_next.start()
    to_prev.start()
    cot_copies = []
    for d in range(1, nx):
        peer = lax.rem(tm + d, nx)
        cot_copies.append(
            remote(cot.at[pl.ds(peer * share, share)], cot_w.at[tm], cot_s.at[d], cot_r.at[d], dev_x(d))
        )
    for copy in cot_copies:
        copy.start()

    def to_time_major(src, dst, first, pairs):
        def body(pair, carry):
            at = first + pair * 32
            left = src[pl.ds(at, 16)].reshape(side, chans)
            right = src[pl.ds(at + 16, 16)].reshape(side, chans)
            moved = mm(perm[...], jnp.concatenate([left, right], axis=1)).astype(BF16)
            start = pl.multiple_of(at, 16)
            dst[:, pl.ds(start, 16), :] = moved[:, :chans].reshape(steps, 16, chans)
            dst[:, pl.ds(start + 16, 16), :] = moved[:, chans:].reshape(steps, 16, chans)
            return carry

        lax.fori_loop(0, pairs, body, 0)

    copy_feat.wait()
    to_time_major(fx, ft, block, rows // 32)
    to_next.wait()
    to_time_major(fx, ft, 0, block // 32)
    to_prev.wait()
    to_time_major(fx, ft, rows + block, block // 32)

    def forward(pair, carry):
        t = pair * 2
        both = jnp.concatenate([ft[t], ft[t + 1]], axis=1)
        mix = (mm(m_mat[0], both) + mm(m_mat[1], both)).astype(BF16)
        for half in range(2):
            mix_one = mix[:, half * chans : (half + 1) * chans]
            mixed[t + half] = mix_one
            pre = mm(mix_one, wg[...])
            gate = 1.0 / (1.0 + jnp.exp(-pre))
            act_t[t + half] = (pre * gate).astype(BF16)
            slope[t + half] = gate * (1.0 + pre * (1.0 - gate))
        return carry

    lax.fori_loop(0, steps // 2, forward, 0)

    def act_rows(at):
        start = pl.multiple_of(at, 16)
        left = act_t[:, pl.ds(start, 16), :].reshape(side, chans)
        right = act_t[:, pl.ds(start + 16, 16), :].reshape(side, chans)
        moved = mm(perm[...], jnp.concatenate([left, right], axis=1)).astype(BF16)
        return moved[:, :chans].reshape(16, steps, chans), moved[:, chans:].reshape(16, steps, chans)

    act_copies = []
    for d in list(range(1, nx)) + [0]:
        peer = lax.rem(tm + d, nx)
        for piece in range(share // 32):
            at = peer * share + piece * 32
            left, right = act_rows(at)
            if d == 0:
                act_w[tm, pl.ds(piece * 32, 16)] = left
                act_w[tm, pl.ds(piece * 32 + 16, 16)] = right
            else:
                act_b[d, pl.ds(piece * 32, 16)] = left
                act_b[d, pl.ds(piece * 32 + 16, 16)] = right
        if d:
            copy = remote(act_b.at[d], act_w.at[tm], act_s.at[d], act_r.at[d], dev_x(d))
            copy.start()
            act_copies.append(copy)

    copy_own.wait()
    for copy in cot_copies:
        copy.wait()

    group = 4
    lanes = group * chans

    def wide(src, at):
        cols = []
        for b in range(group):
            cols.append(jnp.concatenate([src[j, at + b] for j in range(nx)], axis=0))
        return jnp.concatenate(cols, axis=1)

    def tiled(table):
        return jnp.concatenate([table] * group, axis=1)

    def inverse(real, imag):
        high, low = split(jnp.concatenate([real, imag], axis=0))
        return mm(inv_tab[...], jnp.concatenate([high, low, high], axis=0))

    def backward(step, carry):
        at = step * group
        for j in range(nx):
            cot_rows = cot_w[j, pl.ds(at, group)].reshape(group * steps, chans)
            conv_rows = mm_t(cot_rows, wo[...], 1, 1).astype(BF16)
            gc_w[j] = conv_rows.reshape(group, steps, chans)
        data = wide(gc_w, 0)
        spec = mm(fwd_tab[...], jnp.concatenate([data, data], axis=0))
        g_freq[step] = spec
        gr, gi = spec[:length], spec[length:]
        k_re, k_im = tiled(kr[...]), tiled(ki[...])
        back = inverse(k_re * gr + k_im * gi, k_re * gi - k_im * gr).astype(BF16)
        for b in range(group):
            for j in range(nx):
                grad_w[j, at + b] = back[j * steps : (j + 1) * steps, b * chans : (b + 1) * chans]
        return carry

    lax.fori_loop(0, share // group, backward, 0)

    grad_copies = []
    for d in range(1, nx):
        peer = lax.rem(tm + d, nx)
        copy = remote(grad_w.at[peer], grad_b.at[pl.ds(tm * share, share)], grd_s.at[d], grd_r.at[d], dev_x(d))
        copy.start()
        grad_copies.append(copy)
    grad_b[pl.ds(tm * share, share)] = grad_w[tm]

    for copy in act_copies:
        copy.wait()

    red_b[...] = jnp.zeros_like(red_b)

    def convolve(step, carry):
        tap_re, tap_im = carry
        at = step * group
        data = wide(act_w, at)
        spec = mm(fwd_tab[...], jnp.concatenate([data, data], axis=0))
        ar, ai = spec[:length], spec[length:]
        k_re, k_im = tiled(kr[...]), tiled(ki[...])
        conv = inverse(k_re * ar - k_im * ai, k_re * ai + k_im * ar).astype(BF16)
        conv_rows = jnp.concatenate([conv[:, b * chans : (b + 1) * chans] for b in range(group)], axis=0)
        cot_cols = wide(cot_w, at)
        cot_rows = jnp.concatenate([cot_cols[:, b * chans : (b + 1) * chans] for b in range(group)], axis=0)
        red_b[pl.ds(0, chans), :] += mm_t(conv_rows, cot_rows, 0, 0)
        gr, gi = g_freq[step, pl.ds(0, length), :], g_freq[step, pl.ds(length, length), :]
        p_re = ar * gr + ai * gi
        p_im = ar * gi - ai * gr
        for b in range(group):
            tap_re = tap_re + p_re[:, b * chans : (b + 1) * chans]
            tap_im = tap_im + p_im[:, b * chans : (b + 1) * chans]
        return tap_re, tap_im

    zero = jnp.zeros((length, chans), F32)
    tap_re, tap_im = lax.fori_loop(0, share // group, convolve, (zero, zero))
    red_b[pl.ds(chans, length), :] = inverse(tap_re, tap_im)

    def scatter(red, rs, send, recv):
        size = red.shape[0] // nq
        copies = []
        for d in range(1, nq):
            start = pl.multiple_of(q_at(d) * size, 8)
            copy = remote(red.at[pl.ds(start, size)], rs.at[d], send.at[d], recv.at[d], dev_q(d))
            copy.start()
            copies.append(copy)
        return copies

    def exchange_y(red, rs, copies, buf, send, recv):
        size = red.shape[0] // nq
        for copy in copies:
            copy.wait()
        start = pl.multiple_of(qq * size, 8)
        total = red[pl.ds(start, size), :]
        for d in range(1, nq):
            total = total + rs[d]
        buf[yy] = total
        out = [remote(buf.at[yy], buf.at[yy], send.at[d], recv.at[d], dev_y(d)) for d in range(1, ny)]
        for copy in out:
            copy.start()
        return out

    def exchange_z(last, copies, buf, send, recv):
        for copy in copies:
            copy.wait()
        total = last[0]
        for i in range(1, ny):
            total = total + last[i]
        buf[zz] = total
        out = [remote(buf.at[zz], buf.at[zz], send.at[d], recv.at[d], dev_z(d)) for d in range(1, nz)]
        for copy in out:
            copy.start()
        return out

    def gather(red, last, copies, send, recv):
        size = red.shape[0] // nq
        for copy in copies:
            copy.wait()
        total = last[0]
        for i in range(1, nz):
            total = total + last[i]
        start = pl.multiple_of(qq * size, 8)
        red[pl.ds(start, size), :] = total
        piece = red.at[pl.ds(start, size)]
        out = [remote(piece, piece, send.at[d], recv.at[d], dev_q(d)) for d in range(1, nq)]
        for copy in out:
            copy.start()
        return out

    rs_b_copies = scatter(red_b, rs_b, rsb_s, rsb_r)

    for copy in grad_copies:
        copy.wait()
    to_time_major(grad_b, act_t, 0, rows // 32)
    red_a[...] = jnp.zeros_like(red_a)

    def graph_back(pair, carry):
        t = pair * 2
        rows_two = act_t[pl.ds(t, 2)].reshape(2 * rows, chans).astype(F32)
        slope_two = slope[pl.ds(t, 2)].reshape(2 * rows, chans)
        grad_pre = (rows_two * slope_two).astype(BF16)
        mixed_two = mixed[pl.ds(t, 2)].reshape(2 * rows, chans)
        red_a[...] += mm_t(mixed_two, grad_pre, 0, 0)
        grad_mixed = mm_t(grad_pre, wg[...], 1, 1).astype(BF16)
        both = jnp.concatenate([grad_mixed[:rows], grad_mixed[rows:]], axis=1)
        spread = mm(mt_mat[0], both) + mm(mt_mat[1], both)
        for half in range(2):
            part = spread[:, half * chans : (half + 1) * chans]
            send_prev[t + half] = part[:block].astype(BF16)
            own[t + half] = part[block : block + rows]
            send_next[t + half] = part[block + rows :].astype(BF16)
        return carry

    lax.fori_loop(0, steps // 2, graph_back, 0)
    grad_next = remote(send_next, from_prev, ghalo_s.at[0], ghalo_r.at[0], dev_bus(1))
    grad_prev = remote(send_prev, from_next, ghalo_s.at[1], ghalo_r.at[1], dev_bus(-1))
    grad_next.start()
    grad_prev.start()
    rs_a_copies = scatter(red_a, rs_a, rsa_s, rsa_r)
    y_b_copies = exchange_y(red_b, rs_b, rs_b_copies, y_b, yb_s, yb_r)
    y_a_copies = exchange_y(red_a, rs_a, rs_a_copies, y_a, ya_s, ya_r)
    z_b_copies = exchange_z(y_b, y_b_copies, z_b, zb_s, zb_r)
    z_a_copies = exchange_z(y_a, y_a_copies, z_a, za_s, za_r)

    grad_next.wait()
    grad_prev.wait()
    copy_cot.wait()

    def finish(piece, carry):
        at = pl.multiple_of(piece * 16, 16)
        for half, other in ((0, from_prev), (1, from_next)):
            first = pl.multiple_of(half * block + at, 16)
            total = own[:, pl.ds(first, 16), :] + other[:, pl.ds(at, 16), :].astype(F32)
            high, low = split(total.reshape(side, chans))
            both = mm(perm[...], jnp.concatenate([high, low], axis=1))
            moved = both[:, :chans] + both[:, chans:]
            base = cot_v[pl.ds(first, 16)].reshape(side, chans).astype(F32)
            grad_feat[pl.ds(first, 16)] = (moved + base).astype(BF16).reshape(16, steps, chans)
        return carry

    lax.fori_loop(0, block // 16, finish, 0)

    ag_b_copies = gather(sum_b, z_b, z_b_copies, agb_s, agb_r)
    ag_a_copies = gather(sum_a, z_a, z_a_copies, aga_s, aga_r)
    for copy in ag_b_copies:
        copy.wait()
    grad_out[...] = sum_b[pl.ds(0, chans), :] * scale
    grad_taps[...] = sum_b[pl.ds(chans, length), :] * scale
    for copy in ag_a_copies:
        copy.wait()
    grad_graph[...] = sum_a[...] * scale


def store(*refs):
    sem = refs[8]
    copies = [pltpu.make_async_copy(src, dst, sem.at[i]) for i, (src, dst) in enumerate(zip(refs[:4], refs[4:8]))]
    for copy in copies:
        copy.start()
    for copy in copies:
        copy.wait()


def shards(sizes, features, couplings, neighbors, w_graph, kernel_taps, w_out, cotangent):
    nbus, nx, ny, nz, scale = sizes
    rows, steps, chans = features.shape
    length = kernel_taps.shape[0]
    block = couplings.shape[2]
    share = rows // nx
    nq = nx * CORES
    group = 4
    fwd_tab, inv_tab = dft_tables(length)
    size_a = chans // nq
    size_b = (chans + length) // nq
    vmem = pltpu.VMEM
    dma = pltpu.SemaphoreType.DMA
    in_vmem = pl.BlockSpec(memory_space=pltpu.VMEM)
    in_any = pl.BlockSpec(memory_space=pl.ANY)
    in_hbm = pl.BlockSpec(memory_space=pltpu.HBM)
    scratch = [
        vmem(couplings.shape, BF16),
        pltpu.SMEM(neighbors.shape, jnp.int32),
        vmem(w_graph.shape, BF16),
        vmem(kernel_taps.shape, BF16),
        vmem(w_out.shape, BF16),
        vmem(fwd_tab.shape, BF16),
        vmem(inv_tab.shape, BF16),
        vmem((rows + 2 * block, steps, chans), BF16),
        vmem((steps, rows + 2 * block, chans), BF16),
        vmem((16 * steps, 16 * steps), BF16),
        vmem((2, rows, rows + 2 * block), BF16),
        vmem((2, rows + 2 * block, rows), BF16),
        vmem((steps, rows, chans), BF16),
        vmem((steps, rows, chans), F32),
        vmem((steps, rows, chans), BF16),
        vmem((nx, share, steps, chans), BF16),
        vmem((nx, share, steps, chans), BF16),
        vmem((rows, steps, chans), BF16),
        vmem((nx, share, steps, chans), BF16),
        vmem((nx, group, steps, chans), BF16),
        vmem((share // group, 2 * length, group * chans), F32),
        vmem((length, chans), F32),
        vmem((length, chans), F32),
        vmem((nx, share, steps, chans), BF16),
        vmem((rows, steps, chans), BF16),
        vmem((steps, rows, chans), F32),
        vmem((steps, block, chans), BF16),
        vmem((steps, block, chans), BF16),
        vmem((steps, block, chans), BF16),
        vmem((steps, block, chans), BF16),
        vmem((chans, chans), F32),
        vmem((nq, size_a, chans), F32),
        vmem((ny, size_a, chans), F32),
        vmem((nz, size_a, chans), F32),
        vmem((chans, chans), F32),
        vmem((chans + length, chans), F32),
        vmem((nq, size_b, chans), F32),
        vmem((ny, size_b, chans), F32),
        vmem((nz, size_b, chans), F32),
        vmem((chans + length, chans), F32),
        dma((10,)),
    ]
    for count in (2, nx, nx, nx, 2, nq, nq, ny, ny, nz, nz, nq, nq):
        scratch += [dma((count,)), dma((count,))]
    results = pl.pallas_call(
        functools.partial(kernel, sizes),
        out_shape=(
            jax.ShapeDtypeStruct(features.shape, BF16),
            jax.ShapeDtypeStruct((chans, chans), F32),
            jax.ShapeDtypeStruct((chans, chans), F32),
            jax.ShapeDtypeStruct((length, chans), F32),
        ),
        in_specs=[in_hbm] * 9,
        out_specs=(in_vmem, in_vmem, in_vmem, in_vmem),
        scratch_shapes=scratch,
        compiler_params=pltpu.CompilerParams(
            collective_id=0, has_side_effects=True, vmem_limit_bytes=67043328
        ),
    )(features, cotangent, couplings, neighbors, w_graph, kernel_taps, w_out, jnp.asarray(fwd_tab), jnp.asarray(inv_tab))
    return pl.pallas_call(
        store,
        out_shape=tuple(jax.ShapeDtypeStruct(r.shape, r.dtype) for r in results),
        in_specs=[in_vmem] * 4,
        out_specs=(in_hbm,) * 4,
        scratch_shapes=[dma((4,))],
    )(*results)


def solution(mesh):
    nbus, nx = mesh.shape["bus"], mesh.shape["tm"]
    nz = nbus // (CORES * CHIPS_Y)

    def step(features, couplings, neighbors, w_graph, kernel_taps, w_out, cotangent):
        total_rows = nbus * features.shape[0] * features.shape[1] * nx
        sizes = (nbus, nx, CHIPS_Y, nz, 1.0 / math.sqrt(total_rows))
        return shards(sizes, features, couplings, neighbors, w_graph, kernel_taps, w_out, cotangent)

    return jax.shard_map(
        step,
        mesh=mesh,
        in_specs=(
            P("bus", "tm", None),
            P("bus", None, None, None),
            P("bus", None),
            P(),
            P(),
            P(),
            P("bus", "tm", None),
        ),
        out_specs=(P("bus", "tm", None), P(), P(), P()),
        check_vma=False,
    )
```
